32 devices in a mesh: rep: 8 (over z, y), tp: 4 (over x, core).
Axes of the slice: x: 2, y: 2, z: 4, core: 2. Of those that a mesh axis runs over, the one named last changes fastest.
Arguments:
- tokens: bfloat16 [8192, 8192], P('rep', 'tp'), may hold values from -6 to 6
- grad_out: bfloat16 [8192, 4096], P('rep', 'tp'), may hold values from -0.0625 to 0.0625
- lengths: int32 [8, 4], replicated, may hold values from 0 to 1024, as said below
- master: float32 [8192, 2048], P('rep', 'tp'), may hold values from -3 to 3
- first: float32 [8192, 2048], P('rep', 'tp'), may hold values from -6 to 6
- second: float32 [8192, 2048], P('rep', 'tp'), may hold values from 0.25 to 4
Outputs:
- new_master: float32 [8192, 2048], P('rep', 'tp')
- new_first: float32 [8192, 2048], P('rep', 'tp')
- new_second: float32 [8192, 2048], P('rep', 'tp')
- healthy_weights: bfloat16 [8192, 2048], P(None, 'tp')
- slot_weights: bfloat16 [8, 8192, 4096], P('rep', None, 'tp')
The draws below stay inside these ranges and needn't reach their ends.
Inputs may be any that keep to these rules, and one draw needn't show every extreme that they name: `lengths`: each row is one replica's split of the 2048 columns over its devices in tp order: the entries are multiples of 256, sum to 2048, the nonzero ones come first and number at least half of the row; a row is either all 512 or has an entry equal to 1024, and some row has an entry equal to 1024.
All inputs are finite; a program needn't handle non-finite values.
Results may differ from the reference program's by a relative error of at most 0.0019.
Values may be sent and summed in bfloat16 or wider, within the bound.
A program may use at most 128 MiB of HBM per device.

```python
import math
import jax
import jax.numpy as jnp
from jax import lax

D = 8192
COLS = 2048
TOK_DEV = 1024
STEP = 1000
TOKENS = 8192
MAXLEN = 1024
N_REP = 8
N_TP = 4


def replica_split(key, counts):
    key_largest, key_order = jax.random.split(key)
    unit_width = COLS // (2 * N_TP)
    position = jnp.arange(N_TP, dtype=jnp.int32)
    largest = jax.random.randint(key_largest, (), 0, counts)
    scores = jax.random.permutation(key_order, N_TP)
    active = position < counts
    others = active & (position != largest)
    order_rank = jnp.sum(others[None, :] & (scores[None, :] < scores[:, None]), axis=1)
    spare_units = 2 * N_TP - 4 - (counts - 1)
    extra_units = jnp.clip(spare_units - 3 * order_rank, 0, 3)
    unit_counts = jnp.where(position == largest, 4, jnp.where(others, 1 + extra_units, 0))
    unit_counts = jnp.where(counts == N_TP, 2, unit_counts)
    return (unit_counts * unit_width).astype(jnp.int32)


def draw_lengths(key, part):
    keys = jax.random.split(jax.random.fold_in(key, 17), 3)
    counts = jax.random.randint(keys[0], (N_REP,), N_TP // 2, N_TP + 1)
    forced = jax.random.randint(keys[1], (), 0, N_REP)
    counts = jnp.where(jnp.arange(N_REP) == forced, N_TP // 2, counts)
    return jax.vmap(replica_split)(jax.random.split(keys[2], N_REP), counts)


def block_scale(key, dims, cuts, smallest, high):
    gain = 1.0
    for axis_at, shards_of in cuts:
        heights = jax.random.uniform(jax.random.fold_in(jax.random.fold_in(key, 6), axis_at), (shards_of,), jnp.float32, smallest / len(cuts), high / len(cuts))
        gain = gain * jnp.repeat(jnp.exp(heights), dims[axis_at] // shards_of).reshape((-1,) + (1,) * (len(dims) - 1 - axis_at))
    return gain


def gaussian(stream_key, dims, scale, reach, cuts=(), kind=jnp.bfloat16):
    level = block_scale(stream_key, dims, cuts, -0.22, 0.18) if cuts else 1.0
    array = jax.random.normal(stream_key, dims, jnp.float32) * scale * level
    return jnp.minimum(jnp.maximum(array, -reach), reach).astype(kind)


def setup_inputs(seed: int = 0) -> dict:
    arg_keys = jax.random.split(jax.random.key(seed), 7)
    tokens = gaussian(arg_keys[0], (TOKENS, D), 1.0, 6.0, ((0, 8), (1, 4)))
    grad_out = gaussian(arg_keys[1], (TOKENS, N_TP * MAXLEN), (TOK_DEV * N_REP) ** -0.5, 0.0625, ((0, 8), (1, 4)))
    lengths = draw_lengths(jax.random.fold_in(arg_keys[6], 71), 0)
    master = gaussian(arg_keys[3], (D, COLS), 0.5, 3.0, ((0, 8), (1, 4)), jnp.float32)
    first = gaussian(arg_keys[4], (D, COLS), 1.0, 6.0, ((0, 8), (1, 4)), jnp.float32)
    second = jnp.clip(jnp.exp(math.log(4.0) - 2.7725887 * jax.random.uniform(arg_keys[5], (D, COLS), jnp.float32) ** block_scale(arg_keys[5], (D, COLS), ((0, 8), (1, 4)), -0.2, 0.2)), 0.25, 4.0)
    return {"tokens": tokens, "grad_out": grad_out, "lengths": lengths, "master": master, "first": first, "second": second}


decay_first = 0.9
decay_second = 0.999
learning_rate = 0.02
weight_decay = 0.1
epsilon = 1e-08

def source(row_lengths, begins):
    columns = jnp.arange(COLS, dtype=jnp.int32)
    inside = (begins[None, :] <= columns[:, None]) & (columns[:, None] < (begins + row_lengths)[None, :])
    slot_index = jnp.arange(N_TP, dtype=jnp.int32)[None, :] * MAXLEN + columns[:, None] - begins[None, :]
    return lax.optimization_barrier(jnp.sum(jnp.where(inside, slot_index, 0), axis=1)).astype(jnp.int32)

def adam_update(master, first, second, gradient):
    scale_first = 1.0 - decay_first ** STEP
    scale_second = 1.0 - decay_second ** STEP
    new_first = decay_first * first + (1.0 - decay_first) * gradient
    new_second = decay_second * second + (1.0 - decay_second) * gradient * gradient
    direction = new_first / scale_first / (jnp.sqrt(new_second / scale_second) + epsilon)
    new_master = master - learning_rate * (direction + weight_decay * master)
    return (new_master, new_first, new_second)

def reference(tokens, grad_out, lengths, master, first, second):
    lengths = lengths.astype(jnp.int32)
    starts = (jnp.cumsum(lengths, axis=1) - lengths).astype(jnp.int32)
    token_blocks = tokens.reshape(N_REP, TOK_DEV, D)
    output_blocks = grad_out.reshape(N_REP, TOK_DEV, N_TP * MAXLEN)

    def accumulate(running, member):
        token_rows, grad_rows, row_lengths, begins = member
        dense_grad = jnp.take(grad_rows, source(row_lengths, begins), axis=1)
        return (running + jnp.dot(token_rows.T, dense_grad, preferred_element_type=jnp.float32), None)
    gradient = lax.scan(accumulate, jnp.zeros((D, COLS), jnp.float32), (token_blocks, output_blocks, lengths, starts))[0]
    new_master, new_first, new_second = adam_update(master, first, second, gradient)
    weights = new_master.astype(jnp.bfloat16)
    slot_pos = jnp.arange(N_TP * MAXLEN, dtype=jnp.int32)
    owner = (slot_pos // MAXLEN).astype(jnp.int32)
    within = (slot_pos % MAXLEN).astype(jnp.int32)

    def layout(member):
        row_lengths, begins = member
        column_src = (jnp.take(begins, owner) + within).astype(jnp.int32)
        valid = within < jnp.take(row_lengths, owner)
        picked = jnp.take(weights, jnp.clip(column_src, 0, COLS - 1), axis=1)
        return jnp.where(valid[None, :], picked, jnp.zeros_like(picked))
    slot_weights = lax.map(layout, (lengths, starts))
    return (new_master, new_first, new_second, weights, slot_weights)
```

```python
import jax
import jax.numpy as jnp
from jax import lax
from jax.experimental import pallas as pl
from jax.experimental.pallas import tpu as pltpu
from jax.sharding import PartitionSpec as P

COLS = 2048
STEP = 1000


decay_first = 0.9
decay_second = 0.999
learning_rate = 0.02
weight_decay = 0.1
epsilon = 1e-08


def adam_update(master, first, second, gradient):
    scale_first = 1.0 - decay_first**STEP
    scale_second = 1.0 - decay_second**STEP
    new_first = decay_first * first + (1.0 - decay_first) * gradient
    new_second = decay_second * second + (1.0 - decay_second) * gradient * gradient
    direction = new_first / scale_first / (jnp.sqrt(new_second / scale_second) + epsilon)
    new_master = master - learning_rate * (direction + weight_decay * master)
    return (new_master, new_first, new_second)


def on_device_general(tokens, grad_out, lengths, master, first, second):
    shards = lax.axis_size("tp")
    replicas = lax.axis_size("rep")
    column_index = lax.axis_index("tp")
    replica_index = lax.axis_index("rep")
    token_count = tokens.shape[0]
    slot_width = grad_out.shape[1]
    block_width = COLS // shards
    begins_all = jnp.cumsum(lengths, axis=1) - lengths
    is_mine = jnp.arange(shards, dtype=jnp.int32) == column_index
    own_lengths = lax.dynamic_index_in_dim(lengths, replica_index, 0, keepdims=False)
    own_begins = lax.dynamic_index_in_dim(begins_all, replica_index, 0, keepdims=False)
    my_begin = jnp.sum(jnp.where(is_mine, own_begins, 0))
    my_length = jnp.sum(jnp.where(is_mine, own_lengths, 0))
    columns = jnp.arange(COLS, dtype=jnp.int32)
    offset = columns - my_begin
    inside = (offset >= 0) & (offset < my_length)
    picked = jnp.take(grad_out, jnp.clip(offset, 0, slot_width - 1), axis=1)
    spread = jnp.where(inside[None, :], picked, jnp.zeros_like(picked)).reshape(
        token_count, shards, block_width
    )
    received = lax.all_to_all(spread, "tp", split_axis=1, concat_axis=1, tiled=True)
    grad_block = jnp.sum(received, axis=1)
    grad_columns = lax.dot_general(
        lax.all_gather(tokens, "tp", axis=1, tiled=True),
        grad_block,
        (((0,), (0,)), ((), ())),
        preferred_element_type=jnp.float32,
    )
    summed = lax.psum_scatter(
        grad_columns.astype(jnp.bfloat16), "rep", scatter_dimension=0, tiled=True
    ).astype(jnp.float32)
    new_master, new_first, new_second = adam_update(master, first, second, summed)
    weights = new_master.astype(jnp.bfloat16)
    healthy = lax.all_gather(weights, "rep", axis=0, tiled=True)
    replica_rows = lax.all_gather(weights, "tp", axis=1, tiled=True)
    slot_begins = jnp.sum(jnp.where(is_mine[None, :], begins_all, 0), axis=1)
    slot_lengths = jnp.sum(jnp.where(is_mine[None, :], lengths, 0), axis=1)
    within = jnp.arange(slot_width, dtype=jnp.int32)
    source_cols = slot_begins[:, None] + within[None, :]
    valid = within[None, :] < slot_lengths[:, None]
    taken = jnp.take(replica_rows, jnp.clip(source_cols, 0, COLS - 1).reshape(-1), axis=1)
    outgoing = jnp.where(valid.reshape(-1)[None, :], taken, jnp.zeros_like(taken))
    outgoing = outgoing.reshape(replica_rows.shape[0], replicas, slot_width)
    arrived = lax.all_to_all(outgoing, "rep", split_axis=1, concat_axis=0, tiled=True)
    slot_weights = arrived.reshape(1, -1, slot_width)
    return (new_master, new_first, new_second, healthy, slot_weights)


def unit_tables(lengths, unit, slot_units, total_units):
    shards = lax.axis_size("tp")
    begins_all = jnp.cumsum(lengths, axis=1) - lengths
    own_lengths = lax.dynamic_index_in_dim(lengths, lax.axis_index("rep"), 0, keepdims=False) // unit
    own_begins = lax.dynamic_index_in_dim(begins_all, lax.axis_index("rep"), 0, keepdims=False) // unit
    column = jnp.arange(total_units, dtype=jnp.int32)[:, None]
    inside = (own_begins[None, :] <= column) & (column < (own_begins + own_lengths)[None, :])
    place = jnp.arange(shards, dtype=jnp.int32)[None, :] * slot_units + column - own_begins[None, :]
    source = jnp.sum(jnp.where(inside, place, 0), axis=1)
    mine = jnp.arange(shards, dtype=jnp.int32) == lax.axis_index("tp")
    my_begin = jnp.sum(jnp.where(mine, own_begins, 0))
    my_length = jnp.sum(jnp.where(mine, own_lengths, 0))
    within = jnp.arange(slot_units, dtype=jnp.int32)
    slot_unit = jnp.clip(my_begin + within, 0, total_units - 1)
    valid = (within < my_length).astype(jnp.int32)
    me = jnp.full((1,), lax.axis_index("tp"), jnp.int32)
    return source.astype(jnp.int32), jnp.concatenate([slot_unit, valid, me]).astype(jnp.int32)


def partial_product(source, tokens, slots, unit, block_width):
    rows, features = tokens.shape
    per_block = block_width // unit
    slot_units = slots.shape[2] // unit
    blocks = source.shape[0] // per_block
    tile = min(512, features)

    def body(source_ref, tokens_ref, *refs):
        out_ref = refs[-1]
        for p in range(per_block):
            out_ref[0, :, p * unit : (p + 1) * unit] = lax.dot_general(
                tokens_ref[...], refs[p][0], (((0,), (0,)), ((), ())), preferred_element_type=jnp.float32
            ).astype(out_ref.dtype)

    def unit_spec(p):
        def index(j, f, source_ref):
            at = source_ref[j * per_block + p]
            return (at // slot_units, 0, at % slot_units)

        return pl.BlockSpec((1, rows, unit), index)

    return pl.pallas_call(
        body,
        out_shape=jax.ShapeDtypeStruct((blocks, features, block_width), jnp.bfloat16),
        grid_spec=pltpu.PrefetchScalarGridSpec(
            num_scalar_prefetch=1,
            grid=(blocks, features // tile),
            in_specs=[pl.BlockSpec((rows, tile), lambda j, f, s: (0, f))] + [unit_spec(p) for p in range(per_block)],
            out_specs=pl.BlockSpec((1, tile, block_width), lambda j, f, s: (j, f, 0)),
        ),
    )(source, tokens, *([slots] * per_block))


def place_weights(table, blocks, unit, slot_units, replicas, shards):
    _, rows, block_width = blocks.shape
    per_block = block_width // unit

    def body(table_ref, own_ref, *refs):
        healthy_ref, slot_ref = refs[-2:]
        healthy_ref[...] = own_ref[0]
        for s in range(slot_units):
            keep = table_ref[slot_units + s] > 0
            value = refs[s][0]
            slot_ref[0, :, s * unit : (s + 1) * unit] = jnp.where(keep, value, jnp.zeros_like(value))

    def unit_spec(s):
        def index(r, table_ref):
            at = table_ref[s]
            return (r * shards + at // per_block, 0, at % per_block)

        return pl.BlockSpec((1, rows, unit), index)

    return pl.pallas_call(
        body,
        out_shape=(
            jax.ShapeDtypeStruct((replicas * rows, block_width), blocks.dtype),
            jax.ShapeDtypeStruct((1, replicas * rows, slot_units * unit), blocks.dtype),
        ),
        grid_spec=pltpu.PrefetchScalarGridSpec(
            num_scalar_prefetch=1,
            grid=(replicas,),
            in_specs=[pl.BlockSpec((1, rows, block_width), lambda r, t: (r * shards + t[2 * slot_units], 0, 0))]
            + [unit_spec(s) for s in range(slot_units)],
            out_specs=(
                pl.BlockSpec((rows, block_width), lambda r, t: (r, 0)),
                pl.BlockSpec((1, rows, slot_units * unit), lambda r, t: (0, r, 0)),
            ),
        ),
    )(table, *([blocks] * (slot_units + 1)))


def on_device(tokens, grad_out, lengths, master, first, second):
    shards = lax.axis_size("tp")
    replicas = lax.axis_size("rep")
    rows, block_width = master.shape
    unit = COLS // (2 * shards)
    slot_units = grad_out.shape[1] // unit
    row_blocks = replicas // shards
    source, table = unit_tables(lengths, unit, slot_units, COLS // unit)
    slots = lax.all_gather(grad_out, "tp")
    partial = partial_product(source, tokens, slots, unit, block_width)
    chunk = lax.psum_scatter(
        partial.reshape(replicas * rows, block_width), "rep", scatter_dimension=0, tiled=True
    )
    moves = [
        (k * shards + j, (row_blocks * j + k % row_blocks) * shards + k // row_blocks)
        for k in range(replicas)
        for j in range(shards)
    ]
    summed = lax.ppermute(chunk, ("rep", "tp"), moves).astype(jnp.float32)
    new_master, new_first, new_second = adam_update(master, first, second, summed)
    weights = new_master.astype(jnp.bfloat16)
    blocks = lax.all_gather(weights, ("rep", "tp"))
    healthy, slot_weights = place_weights(table, blocks, unit, slot_units, replicas, shards)
    return (new_master, new_first, new_second, healthy, slot_weights)


def solution(mesh):
    placed = (P("rep", "tp"), P("rep", "tp"), P(), P("rep", "tp"), P("rep", "tp"), P("rep", "tp"))
    shards, replicas = mesh.shape["tp"], mesh.shape["rep"]
    by_units = (COLS // (2 * shards)) % 128 == 0 and replicas % shards == 0
    return jax.shard_map(
        on_device if by_units else on_device_general,
        mesh=mesh,
        in_specs=placed,
        out_specs=(
            P("rep", "tp"),
            P("rep", "tp"),
            P("rep", "tp"),
            P(None, "tp"),
            P("rep", None, "tp"),
        ),
        check_vma=False,
    )
```

```python
import functools

import jax
import jax.numpy as jnp
from jax import lax
from jax.experimental import pallas as pl
from jax.experimental.pallas import tpu as pltpu
from jax.sharding import PartitionSpec as P

COLS = 2048
STEP = 1000


decay_first = 0.9
decay_second = 0.999
learning_rate = 0.02
weight_decay = 0.1
epsilon = 1e-08
MESH = pl.DeviceIdType.MESH


def adam_update(master, first, second, gradient):
    scale_first = 1.0 - decay_first**STEP
    scale_second = 1.0 - decay_second**STEP
    new_first = decay_first * first + (1.0 - decay_first) * gradient
    new_second = decay_second * second + (1.0 - decay_second) * gradient * gradient
    direction = new_first / scale_first / (jnp.sqrt(new_second / scale_second) + epsilon)
    new_master = master - learning_rate * (direction + weight_decay * master)
    return (new_master, new_first, new_second)


def on_device_general(tokens, grad_out, lengths, master, first, second):
    shards = lax.axis_size("tp")
    replicas = lax.axis_size("rep")
    column_index = lax.axis_index("tp")
    replica_index = lax.axis_index("rep")
    token_count = tokens.shape[0]
    slot_width = grad_out.shape[1]
    block_width = COLS // shards
    begins_all = jnp.cumsum(lengths, axis=1) - lengths
    is_mine = jnp.arange(shards, dtype=jnp.int32) == column_index
    own_lengths = lax.dynamic_index_in_dim(lengths, replica_index, 0, keepdims=False)
    own_begins = lax.dynamic_index_in_dim(begins_all, replica_index, 0, keepdims=False)
    my_begin = jnp.sum(jnp.where(is_mine, own_begins, 0))
    my_length = jnp.sum(jnp.where(is_mine, own_lengths, 0))
    columns = jnp.arange(COLS, dtype=jnp.int32)
    offset = columns - my_begin
    inside = (offset >= 0) & (offset < my_length)
    picked = jnp.take(grad_out, jnp.clip(offset, 0, slot_width - 1), axis=1)
    spread = jnp.where(inside[None, :], picked, jnp.zeros_like(picked)).reshape(
        token_count, shards, block_width
    )
    received = lax.all_to_all(spread, "tp", split_axis=1, concat_axis=1, tiled=True)
    grad_block = jnp.sum(received, axis=1)
    grad_columns = lax.dot_general(
        lax.all_gather(tokens, "tp", axis=1, tiled=True),
        grad_block,
        (((0,), (0,)), ((), ())),
        preferred_element_type=jnp.float32,
    )
    summed = lax.psum_scatter(
        grad_columns.astype(jnp.bfloat16), "rep", scatter_dimension=0, tiled=True
    ).astype(jnp.float32)
    new_master, new_first, new_second = adam_update(master, first, second, summed)
    weights = new_master.astype(jnp.bfloat16)
    healthy = lax.all_gather(weights, "rep", axis=0, tiled=True)
    replica_rows = lax.all_gather(weights, "tp", axis=1, tiled=True)
    slot_begins = jnp.sum(jnp.where(is_mine[None, :], begins_all, 0), axis=1)
    slot_lengths = jnp.sum(jnp.where(is_mine[None, :], lengths, 0), axis=1)
    within = jnp.arange(slot_width, dtype=jnp.int32)
    source_cols = slot_begins[:, None] + within[None, :]
    valid = within[None, :] < slot_lengths[:, None]
    taken = jnp.take(replica_rows, jnp.clip(source_cols, 0, COLS - 1).reshape(-1), axis=1)
    outgoing = jnp.where(valid.reshape(-1)[None, :], taken, jnp.zeros_like(taken))
    outgoing = outgoing.reshape(replica_rows.shape[0], replicas, slot_width)
    arrived = lax.all_to_all(outgoing, "rep", split_axis=1, concat_axis=0, tiled=True)
    slot_weights = arrived.reshape(1, -1, slot_width)
    return (new_master, new_first, new_second, healthy, slot_weights)


def unit_tables(lengths, unit, slot_units, total_units):
    shards = lax.axis_size("tp")
    begins_all = jnp.cumsum(lengths, axis=1) - lengths
    own_lengths = lax.dynamic_index_in_dim(lengths, lax.axis_index("rep"), 0, keepdims=False) // unit
    own_begins = lax.dynamic_index_in_dim(begins_all, lax.axis_index("rep"), 0, keepdims=False) // unit
    column = jnp.arange(total_units, dtype=jnp.int32)[:, None]
    inside = (own_begins[None, :] <= column) & (column < (own_begins + own_lengths)[None, :])
    place = jnp.arange(shards, dtype=jnp.int32)[None, :] * slot_units + column - own_begins[None, :]
    source = jnp.sum(jnp.where(inside, place, 0), axis=1)
    mine = jnp.arange(shards, dtype=jnp.int32) == lax.axis_index("tp")
    my_begin = jnp.sum(jnp.where(mine, own_begins, 0))
    my_length = jnp.sum(jnp.where(mine, own_lengths, 0))
    within = jnp.arange(slot_units, dtype=jnp.int32)
    slot_unit = jnp.clip(my_begin + within, 0, total_units - 1)
    valid = (within < my_length).astype(jnp.int32)
    me = jnp.full((1,), lax.axis_index("tp"), jnp.int32)
    return source.astype(jnp.int32), jnp.concatenate([slot_unit, valid, me]).astype(jnp.int32)


def partial_product(source, tokens, slots, unit, block_width):
    rows, features = tokens.shape
    per_block = block_width // unit
    slot_units = slots.shape[2] // unit
    blocks = source.shape[0] // per_block
    tile = min(512, features)

    def body(source_ref, tokens_ref, *refs):
        out_ref = refs[-1]
        for p in range(per_block):
            out_ref[0, :, p * unit : (p + 1) * unit] = lax.dot_general(
                tokens_ref[...], refs[p][0], (((0,), (0,)), ((), ())), preferred_element_type=jnp.float32
            ).astype(out_ref.dtype)

    def unit_spec(p):
        def index(j, f, source_ref):
            at = source_ref[j * per_block + p]
            return (at // slot_units, 0, at % slot_units)

        return pl.BlockSpec((1, rows, unit), index)

    return pl.pallas_call(
        body,
        out_shape=jax.ShapeDtypeStruct((blocks, features, block_width), jnp.bfloat16),
        grid_spec=pltpu.PrefetchScalarGridSpec(
            num_scalar_prefetch=1,
            grid=(blocks, features // tile),
            in_specs=[pl.BlockSpec((rows, tile), lambda j, f, s: (0, f))] + [unit_spec(p) for p in range(per_block)],
            out_specs=pl.BlockSpec((1, tile, block_width), lambda j, f, s: (j, f, 0)),
        ),
    )(source, tokens, *([slots] * per_block))


def place_weights(table, blocks, unit, slot_units, replicas, shards):
    _, rows, block_width = blocks.shape
    per_block = block_width // unit

    def body(table_ref, own_ref, *refs):
        healthy_ref, slot_ref = refs[-2:]
        healthy_ref[...] = own_ref[0]
        for s in range(slot_units):
            keep = table_ref[slot_units + s] > 0
            value = refs[s][0]
            slot_ref[0, :, s * unit : (s + 1) * unit] = jnp.where(keep, value, jnp.zeros_like(value))

    def unit_spec(s):
        def index(r, table_ref):
            at = table_ref[s]
            return (r * shards + at // per_block, 0, at % per_block)

        return pl.BlockSpec((1, rows, unit), index)

    return pl.pallas_call(
        body,
        out_shape=(
            jax.ShapeDtypeStruct((replicas * rows, block_width), blocks.dtype),
            jax.ShapeDtypeStruct((1, replicas * rows, slot_units * unit), blocks.dtype),
        ),
        grid_spec=pltpu.PrefetchScalarGridSpec(
            num_scalar_prefetch=1,
            grid=(replicas,),
            in_specs=[pl.BlockSpec((1, rows, block_width), lambda r, t: (r * shards + t[2 * slot_units], 0, 0))]
            + [unit_spec(s) for s in range(slot_units)],
            out_specs=(
                pl.BlockSpec((rows, block_width), lambda r, t: (r, 0)),
                pl.BlockSpec((1, rows, slot_units * unit), lambda r, t: (0, r, 0)),
            ),
        ),
    )(table, *([blocks] * (slot_units + 1)))


def gather_kernel(halves, shards, chunks, own_ref, all_ref, local_sem, send_sem, recv_sem):
    rep, tp = lax.axis_index("rep"), lax.axis_index("tp")
    c, x, y, z = tp % 2, tp // 2, rep % 2, rep // 2
    step_y, step_x = 1 - 2 * y, 2 * (1 - 2 * x)
    here = (rep, tp)
    side = (rep + (1 - c) * step_y, tp + c * step_x)
    cross = (rep + c * step_y, tp + (1 - c) * step_x)
    far = (rep + step_y, tp + step_x)
    mate = (rep, tp + 1 - 2 * c)
    above, below = (rep + 2, tp), (rep - 2, tp)
    rows = own_ref.shape[0] // chunks

    barrier = pltpu.get_barrier_semaphore()
    for at in (side, cross, mate):
        pl.semaphore_signal(barrier, inc=1, device_id=at, device_id_type=MESH)

    @pl.when(z < halves - 1)
    def _():
        pl.semaphore_signal(barrier, inc=1, device_id=above, device_id_type=MESH)

    @pl.when(z > 0)
    def _():
        pl.semaphore_signal(barrier, inc=1, device_id=below, device_id_type=MESH)

    pl.semaphore_wait(barrier, 3 + jnp.minimum(z, 1) + jnp.minimum(halves - 1 - z, 1))

    spots = [(0, 0)] + [(w, d) for w in range(1, halves) for d in (-1, 1)]
    number = {spot: n for n, spot in enumerate(spots)}

    def place(col, spot, h):
        w, d = spot
        return all_ref.at[(col[0] + 2 * w * d) * shards + col[1], pl.ds(h * rows, rows)]

    def copy(kind, spot, col, h, to, out=None, mine=False):
        out = kind if out is None else out
        at = place(col, spot, h)
        seen = spot
        if kind == 0:
            seen = out_spot(spot, out)
        return pltpu.make_async_remote_copy(
            src_ref=own_ref.at[pl.ds(h * rows, rows)] if mine else at,
            dst_ref=at,
            send_sem=send_sem.at[out, number[spot], h],
            recv_sem=recv_sem.at[kind, number[seen], h],
            device_id=to,
            device_id_type=MESH,
        )

    def out_spot(spot, out):
        w, d = spot
        return (w + 1, -1 if out == 0 else 1)

    def line_sends(spot, h):
        w, d = spot
        mine = w == 0
        sends = [
            (None, copy(1, spot, here, h, side, mine=mine)),
            (None, copy(2, spot, here, h, cross, mine=mine)),
            (None, copy(4, spot, here, h, mate, mine=mine)),
        ]
        if w < halves - 1:
            if d <= 0:
                sends.insert(0, (z < halves - 1, copy(0, spot, here, h, above, out=0, mine=mine)))
            if d >= 0:
                sends.insert(0, (z > 0, copy(0, spot, here, h, below, out=8, mine=mine)))
        return sends

    def side_sends(spot, h):
        return [(None, copy(3, spot, side, h, cross)), (None, copy(5, spot, side, h, mate))]

    def cross_sends(spot, h):
        return [(None, copy(6, spot, cross, h, mate))]

    def far_sends(spot, h):
        return [(None, copy(7, spot, far, h, mate))]

    def arrival(kind, spot, col, h):
        at = place(col, spot, h)
        return pltpu.make_async_remote_copy(
            src_ref=at,
            dst_ref=at,
            send_sem=send_sem.at[0, 0, 0],
            recv_sem=recv_sem.at[kind, number[spot], h],
            device_id=mate,
            device_id_type=MESH,
        )

    def exists(spot):
        w, d = spot
        if w == 0:
            return None
        return z >= w if d < 0 else z < halves - w

    def guarded(condition, act):
        if condition is None:
            act()
        else:
            pl.when(condition)(act)

    def act_on(kind, spot, col, sends):
        def act():
            for h in range(chunks):
                if not (kind == 0 and spot[0] == 0):
                    arrival(kind, spot, col, h).wait_recv()
                for condition, send in sends(spot, h):
                    guarded(condition, send.start)

        guarded(exists(spot), act)

    keep = pltpu.make_async_copy(own_ref, all_ref.at[rep * shards + tp], local_sem)
    for wave in range(halves + 2):
        for spot in spots:
            if spot[0] == wave:
                act_on(0, spot, here, line_sends)
        if wave == 0:
            keep.start()
        for spot in spots:
            if spot[0] == wave - 1:
                act_on(1, spot, side, side_sends)
                act_on(2, spot, cross, cross_sends)
        for spot in spots:
            if spot[0] == wave - 2:
                act_on(3, spot, far, far_sends)

    def finish(spot):
        def act():
            for h in range(chunks):
                for kind, col in ((4, (rep, tp + 1 - 2 * c)), (5, None), (6, None), (7, None)):
                    if kind == 5:
                        col = (rep + c * step_y, tp + 1 - 2 * c + (1 - c) * step_x)
                    if kind == 6:
                        col = (rep + (1 - c) * step_y, tp + 1 - 2 * c + c * step_x)
                    if kind == 7:
                        col = (rep + step_y, tp + 1 - 2 * c + step_x)
                    arrival(kind, spot, col, h).wait_recv()
                for sends in (line_sends, side_sends, cross_sends, far_sends):
                    for condition, send in sends(spot, h):
                        guarded(condition, send.wait_send)

        guarded(exists(spot), act)

    for spot in spots:
        finish(spot)
    keep.wait()


def gather_blocks(weights, shards, replicas, chunks=2):
    halves = replicas // 2
    spots = 2 * halves - 1
    return pl.pallas_call(
        functools.partial(gather_kernel, halves, shards, chunks),
        out_shape=jax.ShapeDtypeStruct((replicas * shards,) + weights.shape, weights.dtype),
        in_specs=[pl.BlockSpec(memory_space=pl.ANY)],
        out_specs=pl.BlockSpec(memory_space=pl.ANY),
        scratch_shapes=[
            pltpu.SemaphoreType.DMA,
            pltpu.SemaphoreType.DMA((9, spots, chunks)),
            pltpu.SemaphoreType.DMA((8, spots, chunks)),
        ],
        compiler_params=pltpu.CompilerParams(collective_id=0, has_side_effects=True),
    )(weights)


def on_device(tokens, grad_out, lengths, master, first, second):
    shards = lax.axis_size("tp")
    replicas = lax.axis_size("rep")
    rows, block_width = master.shape
    unit = COLS // (2 * shards)
    slot_units = grad_out.shape[1] // unit
    row_blocks = replicas // shards
    source, table = unit_tables(lengths, unit, slot_units, COLS // unit)
    slots = lax.all_gather(grad_out, "tp")
    partial = partial_product(source, tokens, slots, unit, block_width)
    chunk = lax.psum_scatter(
        partial.reshape(replicas * rows, block_width), "rep", scatter_dimension=0, tiled=True
    )
    moves = [
        (k * shards + j, (row_blocks * j + k % row_blocks) * shards + k // row_blocks)
        for k in range(replicas)
        for j in range(shards)
    ]
    summed = lax.ppermute(chunk, ("rep", "tp"), moves).astype(jnp.float32)
    new_master, new_first, new_second = adam_update(master, first, second, summed)
    weights = new_master.astype(jnp.bfloat16)
    blocks = gather_blocks(weights, shards, replicas)
    healthy, slot_weights = place_weights(table, blocks, unit, slot_units, replicas, shards)
    return (new_master, new_first, new_second, healthy, slot_weights)


def solution(mesh):
    placed = (P("rep", "tp"), P("rep", "tp"), P(), P("rep", "tp"), P("rep", "tp"), P("rep", "tp"))
    shards, replicas = mesh.shape["tp"], mesh.shape["rep"]
    by_units = (COLS // (2 * shards)) % 128 == 0 and replicas % shards == 0 and shards == 4 and replicas % 2 == 0
    return jax.shard_map(
        on_device if by_units else on_device_general,
        mesh=mesh,
        in_specs=placed,
        out_specs=(
            P("rep", "tp"),
            P("rep", "tp"),
            P("rep", "tp"),
            P(None, "tp"),
            P("rep", None, "tp"),
        ),
        check_vma=False,
    )
```

```python
import functools

import jax
import jax.numpy as jnp
from jax import lax
from jax.experimental import pallas as pl
from jax.experimental.pallas import tpu as pltpu
from jax.sharding import PartitionSpec as P

COLS = 2048
STEP = 1000


decay_first = 0.9
decay_second = 0.999
learning_rate = 0.02
weight_decay = 0.1
epsilon = 1e-08
MESH = pl.DeviceIdType.MESH


def adam_update(master, first, second, gradient):
    scale_first = 1.0 - decay_first**STEP
    scale_second = 1.0 - decay_second**STEP
    new_first = decay_first * first + (1.0 - decay_first) * gradient
    new_second = decay_second * second + (1.0 - decay_second) * gradient * gradient
    direction = new_first / scale_first / (jnp.sqrt(new_second / scale_second) + epsilon)
    new_master = master - learning_rate * (direction + weight_decay * master)
    return (new_master, new_first, new_second)


def on_device_general(tokens, grad_out, lengths, master, first, second):
    shards = lax.axis_size("tp")
    replicas = lax.axis_size("rep")
    column_index = lax.axis_index("tp")
    replica_index = lax.axis_index("rep")
    token_count = tokens.shape[0]
    slot_width = grad_out.shape[1]
    block_width = COLS // shards
    begins_all = jnp.cumsum(lengths, axis=1) - lengths
    is_mine = jnp.arange(shards, dtype=jnp.int32) == column_index
    own_lengths = lax.dynamic_index_in_dim(lengths, replica_index, 0, keepdims=False)
    own_begins = lax.dynamic_index_in_dim(begins_all, replica_index, 0, keepdims=False)
    my_begin = jnp.sum(jnp.where(is_mine, own_begins, 0))
    my_length = jnp.sum(jnp.where(is_mine, own_lengths, 0))
    columns = jnp.arange(COLS, dtype=jnp.int32)
    offset = columns - my_begin
    inside = (offset >= 0) & (offset < my_length)
    picked = jnp.take(grad_out, jnp.clip(offset, 0, slot_width - 1), axis=1)
    spread = jnp.where(inside[None, :], picked, jnp.zeros_like(picked)).reshape(
        token_count, shards, block_width
    )
    received = lax.all_to_all(spread, "tp", split_axis=1, concat_axis=1, tiled=True)
    grad_block = jnp.sum(received, axis=1)
    grad_columns = lax.dot_general(
        lax.all_gather(tokens, "tp", axis=1, tiled=True),
        grad_block,
        (((0,), (0,)), ((), ())),
        preferred_element_type=jnp.float32,
    )
    summed = lax.psum_scatter(
        grad_columns.astype(jnp.bfloat16), "rep", scatter_dimension=0, tiled=True
    ).astype(jnp.float32)
    new_master, new_first, new_second = adam_update(master, first, second, summed)
    weights = new_master.astype(jnp.bfloat16)
    healthy = lax.all_gather(weights, "rep", axis=0, tiled=True)
    replica_rows = lax.all_gather(weights, "tp", axis=1, tiled=True)
    slot_begins = jnp.sum(jnp.where(is_mine[None, :], begins_all, 0), axis=1)
    slot_lengths = jnp.sum(jnp.where(is_mine[None, :], lengths, 0), axis=1)
    within = jnp.arange(slot_width, dtype=jnp.int32)
    source_cols = slot_begins[:, None] + within[None, :]
    valid = within[None, :] < slot_lengths[:, None]
    taken = jnp.take(replica_rows, jnp.clip(source_cols, 0, COLS - 1).reshape(-1), axis=1)
    outgoing = jnp.where(valid.reshape(-1)[None, :], taken, jnp.zeros_like(taken))
    outgoing = outgoing.reshape(replica_rows.shape[0], replicas, slot_width)
    arrived = lax.all_to_all(outgoing, "rep", split_axis=1, concat_axis=0, tiled=True)
    slot_weights = arrived.reshape(1, -1, slot_width)
    return (new_master, new_first, new_second, healthy, slot_weights)


def unit_tables(lengths, unit, slot_units, total_units):
    shards = lax.axis_size("tp")
    begins_all = jnp.cumsum(lengths, axis=1) - lengths
    own_lengths = lax.dynamic_index_in_dim(lengths, lax.axis_index("rep"), 0, keepdims=False) // unit
    own_begins = lax.dynamic_index_in_dim(begins_all, lax.axis_index("rep"), 0, keepdims=False) // unit
    column = jnp.arange(total_units, dtype=jnp.int32)[:, None]
    inside = (own_begins[None, :] <= column) & (column < (own_begins + own_lengths)[None, :])
    place = jnp.arange(shards, dtype=jnp.int32)[None, :] * slot_units + column - own_begins[None, :]
    source = jnp.sum(jnp.where(inside, place, 0), axis=1)
    mine = jnp.arange(shards, dtype=jnp.int32) == lax.axis_index("tp")
    my_begin = jnp.sum(jnp.where(mine, own_begins, 0))
    my_length = jnp.sum(jnp.where(mine, own_lengths, 0))
    within = jnp.arange(slot_units, dtype=jnp.int32)
    slot_unit = jnp.clip(my_begin + within, 0, total_units - 1)
    valid = (within < my_length).astype(jnp.int32)
    me = jnp.full((1,), lax.axis_index("tp"), jnp.int32)
    return source.astype(jnp.int32), jnp.concatenate([slot_unit, valid, me]).astype(jnp.int32)


def partial_product(source, tokens, slots, unit, block_width):
    rows, features = tokens.shape
    per_block = block_width // unit
    slot_units = slots.shape[2] // unit
    blocks = source.shape[0] // per_block
    tile = min(512, features)

    def body(source_ref, tokens_ref, *refs):
        out_ref = refs[-1]
        for p in range(per_block):
            out_ref[0, :, p * unit : (p + 1) * unit] = lax.dot_general(
                tokens_ref[...], refs[p][0], (((0,), (0,)), ((), ())), preferred_element_type=jnp.float32
            ).astype(out_ref.dtype)

    def unit_spec(p):
        def index(j, f, source_ref):
            at = source_ref[j * per_block + p]
            return (at // slot_units, 0, at % slot_units)

        return pl.BlockSpec((1, rows, unit), index)

    return pl.pallas_call(
        body,
        out_shape=jax.ShapeDtypeStruct((blocks, features, block_width), jnp.bfloat16),
        grid_spec=pltpu.PrefetchScalarGridSpec(
            num_scalar_prefetch=1,
            grid=(blocks, features // tile),
            in_specs=[pl.BlockSpec((rows, tile), lambda j, f, s: (0, f))] + [unit_spec(p) for p in range(per_block)],
            out_specs=pl.BlockSpec((1, tile, block_width), lambda j, f, s: (j, f, 0)),
        ),
    )(source, tokens, *([slots] * per_block))


def place_weights(table, blocks, unit, slot_units, replicas, shards):
    _, rows, block_width = blocks.shape
    per_block = block_width // unit

    def body(table_ref, own_ref, *refs):
        healthy_ref, slot_ref = refs[-2:]
        healthy_ref[...] = own_ref[0]
        for s in range(slot_units):
            keep = table_ref[slot_units + s] > 0
            value = refs[s][0]
            slot_ref[0, :, s * unit : (s + 1) * unit] = jnp.where(keep, value, jnp.zeros_like(value))

    def unit_spec(s):
        def index(r, table_ref):
            at = table_ref[s]
            return (r * shards + at // per_block, 0, at % per_block)

        return pl.BlockSpec((1, rows, unit), index)

    return pl.pallas_call(
        body,
        out_shape=(
            jax.ShapeDtypeStruct((replicas * rows, block_width), blocks.dtype),
            jax.ShapeDtypeStruct((1, replicas * rows, slot_units * unit), blocks.dtype),
        ),
        grid_spec=pltpu.PrefetchScalarGridSpec(
            num_scalar_prefetch=1,
            grid=(replicas,),
            in_specs=[pl.BlockSpec((1, rows, block_width), lambda r, t: (r * shards + t[2 * slot_units], 0, 0))]
            + [unit_spec(s) for s in range(slot_units)],
            out_specs=(
                pl.BlockSpec((rows, block_width), lambda r, t: (r, 0)),
                pl.BlockSpec((1, rows, slot_units * unit), lambda r, t: (0, r, 0)),
            ),
        ),
    )(table, *([blocks] * (slot_units + 1)))


def gather_kernel(halves, shards, chunks, own_ref, all_ref, local_sem, send_sem, recv_sem):
    rep, tp = lax.axis_index("rep"), lax.axis_index("tp")
    c, x, y, z = tp % 2, tp // 2, rep % 2, rep // 2
    step_y, step_x = 1 - 2 * y, 2 * (1 - 2 * x)
    here = (rep, tp)
    side = (rep + (1 - c) * step_y, tp + c * step_x)
    cross = (rep + c * step_y, tp + (1 - c) * step_x)
    far = (rep + step_y, tp + step_x)
    mate = (rep, tp + 1 - 2 * c)
    above, below = (rep + 2, tp), (rep - 2, tp)
    rows = own_ref.shape[0] // chunks

    barrier = pltpu.get_barrier_semaphore()
    for at in (side, cross, mate):
        pl.semaphore_signal(barrier, inc=1, device_id=at, device_id_type=MESH)

    @pl.when(z < halves - 1)
    def _():
        pl.semaphore_signal(barrier, inc=1, device_id=above, device_id_type=MESH)

    @pl.when(z > 0)
    def _():
        pl.semaphore_signal(barrier, inc=1, device_id=below, device_id_type=MESH)

    pl.semaphore_wait(barrier, 3 + jnp.minimum(z, 1) + jnp.minimum(halves - 1 - z, 1))

    spots = [(0, 0)] + [(w, d) for w in range(1, halves) for d in (-1, 1)]
    number = {spot: n for n, spot in enumerate(spots)}

    def place(col, spot, h):
        w, d = spot
        return all_ref.at[(col[0] + 2 * w * d) * shards + col[1], pl.ds(h * rows, rows)]

    def copy(kind, spot, col, h, to, out=None, mine=False):
        out = kind if out is None else out
        at = place(col, spot, h)
        seen = spot
        if kind == 0:
            seen = out_spot(spot, out)
        return pltpu.make_async_remote_copy(
            src_ref=own_ref.at[pl.ds(h * rows, rows)] if mine else at,
            dst_ref=at,
            send_sem=send_sem.at[out, number[spot], h],
            recv_sem=recv_sem.at[kind, number[seen], h],
            device_id=to,
            device_id_type=MESH,
        )

    def out_spot(spot, out):
        w, d = spot
        return (w + 1, -1 if out == 0 else 1)

    def line_sends(spot, h):
        w, d = spot
        mine = w == 0
        sends = [
            (None, copy(1, spot, here, h, side, mine=mine)),
            (None, copy(2, spot, here, h, cross, mine=mine)),
            (None, copy(4, spot, here, h, mate, mine=mine)),
        ]
        if w < halves - 1:
            if d <= 0:
                sends.insert(0, (z < halves - 1, copy(0, spot, here, h, above, out=0, mine=mine)))
            if d >= 0:
                sends.insert(0, (z > 0, copy(0, spot, here, h, below, out=8, mine=mine)))
        return sends

    def side_sends(spot, h):
        return [(None, copy(3, spot, side, h, cross)), (None, copy(5, spot, side, h, mate))]

    def cross_sends(spot, h):
        return [(None, copy(6, spot, cross, h, mate))]

    def far_sends(spot, h):
        return [(None, copy(7, spot, far, h, mate))]

    def arrival(kind, spot, col, h):
        at = place(col, spot, h)
        return pltpu.make_async_remote_copy(
            src_ref=at,
            dst_ref=at,
            send_sem=send_sem.at[0, 0, 0],
            recv_sem=recv_sem.at[kind, number[spot], h],
            device_id=mate,
            device_id_type=MESH,
        )

    def exists(spot):
        w, d = spot
        if w == 0:
            return None
        return z >= w if d < 0 else z < halves - w

    def guarded(condition, act):
        if condition is None:
            act()
        else:
            pl.when(condition)(act)

    def act_on(kind, spot, col, sends):
        def act():
            for h in range(chunks):
                if not (kind == 0 and spot[0] == 0):
                    arrival(kind, spot, col, h).wait_recv()
                for condition, send in sends(spot, h):
                    guarded(condition, send.start)

        guarded(exists(spot), act)

    keep = pltpu.make_async_copy(own_ref, all_ref.at[rep * shards + tp], local_sem)
    for wave in range(halves + 2):
        for spot in spots:
            if spot[0] == wave:
                act_on(0, spot, here, line_sends)
        if wave == 0:
            keep.start()
        for spot in spots:
            if spot[0] == wave - 1:
                act_on(1, spot, side, side_sends)
                act_on(2, spot, cross, cross_sends)
        for spot in spots:
            if spot[0] == wave - 2:
                act_on(3, spot, far, far_sends)

    def finish(spot):
        def act():
            for h in range(chunks):
                for kind, col in ((4, (rep, tp + 1 - 2 * c)), (5, None), (6, None), (7, None)):
                    if kind == 5:
                        col = (rep + c * step_y, tp + 1 - 2 * c + (1 - c) * step_x)
                    if kind == 6:
                        col = (rep + (1 - c) * step_y, tp + 1 - 2 * c + c * step_x)
                    if kind == 7:
                        col = (rep + step_y, tp + 1 - 2 * c + step_x)
                    arrival(kind, spot, col, h).wait_recv()
                for sends in (line_sends, side_sends, cross_sends, far_sends):
                    for condition, send in sends(spot, h):
                        guarded(condition, send.wait_send)

        guarded(exists(spot), act)

    for spot in spots:
        finish(spot)
    keep.wait()


def gather_blocks(weights, shards, replicas, chunks=2):
    halves = replicas // 2
    spots = 2 * halves - 1
    return pl.pallas_call(
        functools.partial(gather_kernel, halves, shards, chunks),
        out_shape=jax.ShapeDtypeStruct((replicas * shards,) + weights.shape, weights.dtype),
        in_specs=[pl.BlockSpec(memory_space=pl.ANY)],
        out_specs=pl.BlockSpec(memory_space=pl.ANY),
        scratch_shapes=[
            pltpu.SemaphoreType.DMA,
            pltpu.SemaphoreType.DMA((9, spots, chunks)),
            pltpu.SemaphoreType.DMA((8, spots, chunks)),
        ],
        compiler_params=pltpu.CompilerParams(collective_id=0, has_side_effects=True),
    )(weights)


def on_device(tokens, grad_out, lengths, master, first, second):
    shards = lax.axis_size("tp")
    replicas = lax.axis_size("rep")
    rows, block_width = master.shape
    unit = COLS // (2 * shards)
    slot_units = grad_out.shape[1] // unit
    row_blocks = replicas // shards
    source, table = unit_tables(lengths, unit, slot_units, COLS // unit)
    slots = lax.all_gather(grad_out, "tp")
    order = [(q % 2) * (shards // 2) + q // 2 for q in range(shards)]
    by_block = source.reshape(shards, -1)
    source = jnp.concatenate([by_block[q] for q in order])
    partial = partial_product(source, tokens, slots, unit, block_width)
    chunk = lax.psum_scatter(
        partial.reshape(replicas * rows, block_width), "rep", scatter_dimension=0, tiled=True
    )
    moves = [
        (k * shards + j, (row_blocks * j + k % row_blocks) * shards + order[k // row_blocks])
        for k in range(replicas)
        for j in range(shards)
    ]
    summed = lax.ppermute(chunk, ("rep", "tp"), moves).astype(jnp.float32)
    new_master, new_first, new_second = adam_update(master, first, second, summed)
    weights = new_master.astype(jnp.bfloat16)
    blocks = gather_blocks(weights, shards, replicas)
    healthy, slot_weights = place_weights(table, blocks, unit, slot_units, replicas, shards)
    return (new_master, new_first, new_second, healthy, slot_weights)


def solution(mesh):
    placed = (P("rep", "tp"), P("rep", "tp"), P(), P("rep", "tp"), P("rep", "tp"), P("rep", "tp"))
    shards, replicas = mesh.shape["tp"], mesh.shape["rep"]
    by_units = (COLS // (2 * shards)) % 128 == 0 and replicas % shards == 0 and shards == 4 and replicas % 2 == 0
    return jax.shard_map(
        on_device if by_units else on_device_general,
        mesh=mesh,
        in_specs=placed,
        out_specs=(
            P("rep", "tp"),
            P("rep", "tp"),
            P("rep", "tp"),
            P(None, "tp"),
            P("rep", None, "tp"),
        ),
        check_vma=False,
    )
```
